32 devices in a mesh: gx: 8 (over z, x), gy: 4 (over y, core).
Axes of the slice: x: 2, y: 2, z: 4, core: 2. Of those that a mesh axis runs over, the one named last changes fastest.
Arguments:
- tangent: float32 [128, 64, 512], P('gx', 'gy'), may hold values from -6 to 6
- hessian: bfloat16 [5, 5, 128, 64, 512], P(None, None, 'gx', 'gy'), may hold values from -1.5 to 8, as said below
- kernel_rows: float32 [5, 17], replicated, may hold values from -1 to 1
- kernel_cols: float32 [5, 17], replicated, may hold values from -1 to 1
- kernel_depth: bfloat16 [5, 17], replicated, may hold values from -1 to 1
Outputs:
- hessian_product: float32 [128, 64, 512], P('gx', 'gy')
The draws below stay inside these ranges and needn't reach their ends.
Inputs may be any that keep to these rules, and one draw needn't show every extreme that they name: `hessian`: Off-diagonal entries lie within -1.5 to 1.5; diagonal entries are positive, between 0.3 and 8.
All inputs are finite; a program needn't handle non-finite values.
Results may differ from the reference program's by a relative error of at most 0.0022.
Values sent between devices are 32-bit elements; how exact they have to be, the bound alone decides.
A program may use at most 128 MiB of HBM per device.

```python
import jax
import jax.numpy as jnp
from jax import lax

NZ = 512
RADIUS = 8
DENSITIES = 5
TAPS = 17
NX = 128
NY = 64


def draw_hessian(key, part):
    first_key, second_key = jax.random.split(jax.random.fold_in(key, 17))
    full_shape = (DENSITIES, DENSITIES, NX, NY, NZ)
    diag_shape = (DENSITIES, 1, NX, NY, NZ)
    offdiag = jnp.clip(0.3 * jax.random.normal(first_key, full_shape, jnp.float32), -1.5, 1.5)
    diagonal = jnp.exp(jax.random.uniform(second_key, diag_shape, jnp.float32, jnp.log(0.5), jnp.log(5.0)))
    identity = jnp.eye(DENSITIES, dtype=jnp.float32)[:, :, None, None, None]
    return (offdiag * (1.0 - identity) + diagonal * identity).astype(jnp.bfloat16)


def levels(own_key, dims, cuts, least, high):
    def one(dim, parts):
        steps = jax.random.uniform(jax.random.fold_in(jax.random.fold_in(own_key, 6), dim), (parts,), jnp.float32, least / len(cuts), high / len(cuts))
        return jnp.repeat(jnp.exp(steps), dims[dim] // parts).reshape((-1,) + (1,) * (len(dims) - dim - 1))

    level = one(*cuts[0])
    for cut in cuts[1:]:
        level = level * one(*cut)
    return level


def noise(stream_key, shape, width, limit, shards=(), kind=jnp.bfloat16):
    drawn = width * jax.random.normal(stream_key, shape, jnp.float32)
    if shards:
        drawn = drawn * levels(stream_key, shape, shards, -0.22, 0.18)
    return jnp.clip(drawn, -limit, limit).astype(kind)


def setup_inputs(seed: int = 0) -> dict:
    seeds = jax.random.split(jax.random.key(seed), 6)
    return {
        "tangent": noise(seeds[0], (NX, NY, NZ), 1.0, 6.0, ((0, 8), (1, 4)), jnp.float32),
        "hessian": draw_hessian(jax.random.fold_in(seeds[5], 71), 0),
        "kernel_rows": noise(seeds[2], (DENSITIES, TAPS), 0.24, 1.0, (), jnp.float32),
        "kernel_cols": noise(seeds[3], (DENSITIES, TAPS), 0.24, 1.0, (), jnp.float32),
        "kernel_depth": noise(seeds[4], (DENSITIES, TAPS), 0.24, 1.0),
    }


def lateral_forward(field, weights, axis_number):
    total = jnp.zeros_like(field)
    for shift_tap in range(2 * RADIUS + 1):
        total = total + weights[shift_tap] * jnp.roll(field, RADIUS - shift_tap, axis_number)
    return total


def lateral_transpose(field, weights, axis_number):
    total = jnp.zeros_like(field)
    for shift_tap in range(2 * RADIUS + 1):
        total = total + weights[shift_tap] * jnp.roll(field, shift_tap - RADIUS, axis_number)
    return total


def widen(field):
    rounded = lax.optimization_barrier(field.astype(jnp.bfloat16))
    return rounded.astype(jnp.float32)


def depth_forward(field, weights):
    padded = jnp.pad(field, ((0, 0), (0, 0), (RADIUS, RADIUS)))
    total = jnp.zeros(field.shape, jnp.float32)
    for shift_tap in range(2 * RADIUS + 1):
        total = total + weights[shift_tap].astype(jnp.float32) * padded[:, :, shift_tap:shift_tap + NZ]
    return total


def depth_transpose(field, weights):
    padded = jnp.pad(field, ((0, 0), (0, 0), (RADIUS, RADIUS)))
    total = jnp.zeros(field.shape, jnp.float32)
    for shift_tap in range(2 * RADIUS + 1):
        start = 2 * RADIUS - shift_tap
        total = total + weights[shift_tap].astype(jnp.float32) * padded[:, :, start:start + NZ]
    return total


def reference(tangent, hessian, kernel_rows, kernel_cols, kernel_depth):
    densities = []
    for density in range(DENSITIES):
        field = lateral_forward(tangent, kernel_rows[density], 0)
        field = lateral_forward(field, kernel_cols[density], 1)
        densities.append(depth_forward(widen(field), kernel_depth[density]))
    result = jnp.zeros_like(tangent)
    for density in range(DENSITIES):
        gradient = jnp.zeros_like(tangent)
        for other in range(DENSITIES):
            gradient = gradient + hessian[density, other].astype(jnp.float32) * densities[other]
        field = depth_transpose(widen(gradient), kernel_depth[density])
        field = lateral_transpose(field, kernel_rows[density], 0)
        field = lateral_transpose(field, kernel_cols[density], 1)
        result = result + field
    return result
```

```python
import jax
import jax.numpy as jnp
from jax import lax
from jax.experimental import pallas as pl
from jax.experimental.pallas import tpu as pltpu
from jax.sharding import PartitionSpec as P

RADIUS = 8
DENSITIES = 5
TAPS = 2 * RADIUS + 1
LANES = 128


def padded(cells, sides, width):
    for axis, dim in sides:
        count = lax.axis_size(axis)
        head = lax.slice_in_dim(cells, 0, width, axis=dim)
        tail = lax.slice_in_dim(cells, cells.shape[dim] - width, cells.shape[dim], axis=dim)
        cells = jnp.concatenate(
            [
                lax.ppermute(tail, axis, [(i, (i + 1) % count) for i in range(count)]),
                cells,
                lax.ppermute(head, axis, [((i + 1) % count, i) for i in range(count)]),
            ],
            axis=dim,
        )
    return cells


def from_behind(block, axis, distance):
    devices = range(lax.axis_size(axis))
    route = [((i - distance) % len(devices), i) for i in devices]
    return lax.ppermute(block, axis, route)


def split(value):
    high = value.astype(jnp.bfloat16)
    low = (value - high.astype(jnp.float32)).astype(jnp.bfloat16)
    return high, low


def dot(left, right):
    return jnp.dot(left, right, preferred_element_type=jnp.float32)


def picked(taps, index):
    total = jnp.zeros(index.shape, jnp.float32)
    for tap in range(TAPS):
        weight = jnp.broadcast_to(taps[:, tap : tap + 1], index.shape)
        total = jnp.where(index == tap, weight, total)
    return total


def build_forward(sizes, rows, cols, by_row, by_col, high_ref, low_ref):
    span_rows, span_cols, ext_rows, ext_cols = sizes
    wide = ext_rows * ext_cols
    lane = lax.broadcasted_iota(jnp.int32, (span_rows, wide), 1)
    row_index = lane // ext_cols - lax.broadcasted_iota(jnp.int32, (span_rows, wide), 0)
    lane = lax.broadcasted_iota(jnp.int32, (span_cols, wide), 1)
    col_index = lane % ext_cols - lax.broadcasted_iota(jnp.int32, (span_cols, wide), 0)
    for a in range(DENSITIES):
        by_row[...] = picked(rows[a : a + 1], row_index)
        by_col[...] = picked(cols[a : a + 1], col_index)

        def body(r, carry):
            high, low = split(by_row[pl.ds(r, 1), :] * by_col[...])
            start = pl.multiple_of((a * span_rows + r) * span_cols, span_cols)
            high_ref[pl.ds(start, span_cols), :] = high
            low_ref[pl.ds(start, span_cols), :] = low
            return carry

        lax.fori_loop(0, span_rows, body, 0)


def build_backward(sizes, rows, cols, by_row, by_col, high_ref, low_ref):
    span_rows, span_cols, ext_rows, ext_cols = sizes
    own = span_rows * span_cols
    lane = lax.broadcasted_iota(jnp.int32, (ext_rows, own), 1)
    row_index = lax.broadcasted_iota(jnp.int32, (ext_rows, own), 0) - lane // span_cols
    lane = lax.broadcasted_iota(jnp.int32, (ext_cols, own), 1)
    col_index = lax.broadcasted_iota(jnp.int32, (ext_cols, own), 0) - lane % span_cols
    for a in range(DENSITIES):
        by_row[:, a * own : (a + 1) * own] = picked(rows[a : a + 1], row_index)
        by_col[:, a * own : (a + 1) * own] = picked(cols[a : a + 1], col_index)

    def body(r, carry):
        high, low = split(by_row[pl.ds(r, 1), :] * by_col[...])
        start = pl.multiple_of(r * ext_cols, ext_cols)
        high_ref[pl.ds(start, ext_cols), :] = high
        low_ref[pl.ds(start, ext_cols), :] = low
        return carry

    lax.fori_loop(0, ext_rows, body, 0)


def build_bands(depth_taps, band_ref):
    depth = band_ref.shape[1]
    blocks = depth // LANES
    shape = (LANES, LANES)
    index = lax.broadcasted_iota(jnp.int32, shape, 0) - lax.broadcasted_iota(jnp.int32, shape, 1) + RADIUS
    for a in range(DENSITIES):
        taps = depth_taps[a : a + 1]
        same = picked(taps, index).astype(jnp.bfloat16)
        after = picked(taps, index - LANES).astype(jnp.bfloat16)
        before = picked(taps, index + LANES).astype(jnp.bfloat16)
        for p in range(blocks):
            for q in range(blocks):
                block = {0: same, 1: after, -1: before}.get(q - p, jnp.zeros(shape, jnp.bfloat16))
                band_ref[a, p * LANES : (p + 1) * LANES, q * LANES : (q + 1) * LANES] = block


def compute(sizes, ext_ref, hess_ref, rows_ref, cols_ref, depth_ref, out_ref,
            by_row, by_col, by_row_t, by_col_t, fwd_high, fwd_low, bwd_high, bwd_low, bands,
            hess, low_lat, dens, back_high, back_low, hess_sem):
    fetch = pltpu.make_async_copy(hess_ref, hess, hess_sem)
    fetch.start()
    own = sizes[0] * sizes[1]
    rows, cols = rows_ref[...], cols_ref[...]
    build_forward(sizes, rows, cols, by_row, by_col, fwd_high, fwd_low)
    build_backward(sizes, rows, cols, by_row_t, by_col_t, bwd_high, bwd_low)
    build_bands(depth_ref[...].astype(jnp.float32), bands)
    high, low = split(ext_ref[...])

    def lateral(a, carry):
        part = pl.ds(pl.multiple_of(a * own, own), own)
        left = fwd_high[part, :]
        flat = dot(left, high) + dot(left, low) + dot(fwd_low[part, :], high)
        dens[a] = dot(flat.astype(jnp.bfloat16), bands[a])
        return carry

    lax.fori_loop(0, DENSITIES, lateral, 0)
    fetch.wait()

    def gradient(a, carry):
        part = pl.ds(pl.multiple_of(a * own, own), own)
        step = 16
        def piece(i, inner):
            at = pl.ds(pl.multiple_of(i * step, step), step)
            total = hess[a, 0, at, :].astype(jnp.float32) * dens[0, at, :]
            for b in range(1, DENSITIES):
                total = total + hess[a, b, at, :].astype(jnp.float32) * dens[b, at, :]
            low_lat[at, :] = total.astype(jnp.bfloat16)
            return inner
        lax.fori_loop(0, own // step, piece, 0)
        back = lax.dot_general(low_lat[...], bands[a], (((1,), (1,)), ((), ())),
                               preferred_element_type=jnp.float32)
        back_high[part, :], back_low[part, :] = split(back)
        return carry

    lax.fori_loop(0, DENSITIES, gradient, 0)

    tile = 256
    def spread(i, carry):
        at = pl.ds(pl.multiple_of(i * tile, tile), tile)
        left = bwd_high[at, :]
        out_ref[at, :] = (dot(left, back_high[...]) + dot(left, back_low[...])
                          + dot(bwd_low[at, :], back_high[...]))
        return carry
    lax.fori_loop(0, sizes[2] * sizes[3] // tile, spread, 0)


def per_device(tangent, hessian, kernel_rows, kernel_cols, kernel_depth):
    span_rows, span_cols, depth = tangent.shape
    reach = RADIUS
    ext_rows, ext_cols = span_rows + 2 * reach, span_cols + 2 * reach
    sizes = (span_rows, span_cols, ext_rows, ext_cols)
    own, wide = span_rows * span_cols, ext_rows * ext_cols
    extended = padded(tangent, (("gx", 0), ("gy", 1)), RADIUS).reshape(wide, depth)
    full = pl.BlockSpec(memory_space=pltpu.VMEM)
    bf16, f32 = jnp.bfloat16, jnp.float32
    spread = pl.pallas_call(
        lambda *refs: compute(sizes, *refs),
        out_shape=jax.ShapeDtypeStruct((wide, depth), f32),
        in_specs=[full, pl.BlockSpec(memory_space=pl.ANY), full, full, full],
        out_specs=full,
        scratch_shapes=[
            pltpu.VMEM((span_rows, wide), f32),
            pltpu.VMEM((span_cols, wide), f32),
            pltpu.VMEM((ext_rows, DENSITIES * own), f32),
            pltpu.VMEM((ext_cols, DENSITIES * own), f32),
            pltpu.VMEM((DENSITIES * own, wide), bf16),
            pltpu.VMEM((DENSITIES * own, wide), bf16),
            pltpu.VMEM((wide, DENSITIES * own), bf16),
            pltpu.VMEM((wide, DENSITIES * own), bf16),
            pltpu.VMEM((DENSITIES, depth, depth), bf16),
            pltpu.VMEM((DENSITIES, DENSITIES, own, depth), bf16),
            pltpu.VMEM((own, depth), bf16),
            pltpu.VMEM((DENSITIES, own, depth), f32),
            pltpu.VMEM((DENSITIES * own, depth), bf16),
            pltpu.VMEM((DENSITIES * own, depth), bf16),
            pltpu.SemaphoreType.DMA(()),
        ],
        compiler_params=pltpu.CompilerParams(vmem_limit_bytes=56 << 20),
    )(extended, hessian.reshape(DENSITIES, DENSITIES, own, depth), kernel_rows, kernel_cols, kernel_depth)
    spread = spread.reshape(ext_rows, ext_cols, depth)
    middle = spread[reach : reach + span_rows]
    from_next = from_behind(spread[:reach], "gx", -1)
    from_prev = from_behind(spread[span_rows + reach :], "gx", 1)
    middle = middle.at[span_rows - reach :].add(from_next)
    middle = middle.at[:reach].add(from_prev)
    center = middle[:, reach : reach + span_cols]
    from_right = from_behind(middle[:, :reach], "gy", -1)
    from_left = from_behind(middle[:, span_cols + reach :], "gy", 1)
    center = center.at[:, span_cols - reach :].add(from_right)
    center = center.at[:, :reach].add(from_left)
    return center


def solution(mesh):
    return jax.shard_map(
        per_device,
        mesh=mesh,
        in_specs=(P("gx", "gy", None), P(None, None, "gx", "gy", None), P(), P(), P()),
        out_specs=P("gx", "gy", None),
        check_vma=False,
    )
```

```python
import jax
import jax.numpy as jnp
from jax import lax
from jax.experimental import pallas as pl
from jax.experimental.pallas import tpu as pltpu
from jax.sharding import PartitionSpec as P

RADIUS = 8
DENSITIES = 5
TAPS = 2 * RADIUS + 1
LANES = 128


def split(value):
    high = value.astype(jnp.bfloat16)
    low = (value - high.astype(jnp.float32)).astype(jnp.bfloat16)
    return high, low


def dot(left, right):
    return jnp.dot(left, right, preferred_element_type=jnp.float32)


def picked(taps, index):
    total = jnp.zeros(index.shape, jnp.float32)
    for tap in range(TAPS):
        weight = jnp.broadcast_to(taps[:, tap : tap + 1], index.shape)
        total = jnp.where(index == tap, weight, total)
    return total


def build_forward(sizes, rows, cols, by_row, by_col, high_ref, low_ref):
    span_rows, span_cols, ext_rows, ext_cols = sizes
    wide = ext_rows * ext_cols
    lane = lax.broadcasted_iota(jnp.int32, (span_rows, wide), 1)
    row_index = lane // ext_cols - lax.broadcasted_iota(jnp.int32, (span_rows, wide), 0)
    lane = lax.broadcasted_iota(jnp.int32, (span_cols, wide), 1)
    col_index = lane % ext_cols - lax.broadcasted_iota(jnp.int32, (span_cols, wide), 0)
    for a in range(DENSITIES):
        by_row[...] = picked(rows[a : a + 1], row_index)
        by_col[...] = picked(cols[a : a + 1], col_index)

        def body(r, carry):
            high, low = split(by_row[pl.ds(r, 1), :] * by_col[...])
            start = pl.multiple_of((a * span_rows + r) * span_cols, span_cols)
            high_ref[pl.ds(start, span_cols), :] = high
            low_ref[pl.ds(start, span_cols), :] = low
            return carry

        lax.fori_loop(0, span_rows, body, 0)


def build_backward(sizes, rows, cols, by_row, by_col, high_ref, low_ref):
    span_rows, span_cols, ext_rows, ext_cols = sizes
    own = span_rows * span_cols
    lane = lax.broadcasted_iota(jnp.int32, (ext_rows, own), 1)
    row_index = lax.broadcasted_iota(jnp.int32, (ext_rows, own), 0) - lane // span_cols
    lane = lax.broadcasted_iota(jnp.int32, (ext_cols, own), 1)
    col_index = lax.broadcasted_iota(jnp.int32, (ext_cols, own), 0) - lane % span_cols
    for a in range(DENSITIES):
        by_row[:, a * own : (a + 1) * own] = picked(rows[a : a + 1], row_index)
        by_col[:, a * own : (a + 1) * own] = picked(cols[a : a + 1], col_index)

    def body(r, carry):
        high, low = split(by_row[pl.ds(r, 1), :] * by_col[...])
        start = pl.multiple_of(r * ext_cols, ext_cols)
        high_ref[pl.ds(start, ext_cols), :] = high
        low_ref[pl.ds(start, ext_cols), :] = low
        return carry

    lax.fori_loop(0, ext_rows, body, 0)


def build_bands(depth_taps, band_ref):
    depth = band_ref.shape[1]
    blocks = depth // LANES
    shape = (LANES, LANES)
    index = lax.broadcasted_iota(jnp.int32, shape, 0) - lax.broadcasted_iota(jnp.int32, shape, 1) + RADIUS
    for a in range(DENSITIES):
        taps = depth_taps[a : a + 1]
        same = picked(taps, index).astype(jnp.bfloat16)
        after = picked(taps, index - LANES).astype(jnp.bfloat16)
        before = picked(taps, index + LANES).astype(jnp.bfloat16)
        for p in range(blocks):
            for q in range(blocks):
                block = {0: same, 1: after, -1: before}.get(q - p, jnp.zeros(shape, jnp.bfloat16))
                band_ref[a, p * LANES : (p + 1) * LANES, q * LANES : (q + 1) * LANES] = block


def compute(sizes, counts, tangent_ref, hess_ref, rows_ref, cols_ref, depth_ref, out_ref,
            ext, high, low, by_row, by_col, by_row_t, by_col_t, fwd_high, fwd_low, bwd_high, bwd_low,
            bands, hess, lowered, acc, back_high, back_low, spread, from_left, from_right,
            from_up, from_down, local_sems, send_sems, recv_sems, back_send_sems, back_recv_sems):
    span_rows, span_cols, ext_rows, ext_cols = sizes
    depth = acc.shape[1]
    reach = RADIUS
    own, wide = span_rows * span_cols, ext_rows * ext_cols
    gx, gy = lax.axis_index("gx"), lax.axis_index("gy")
    up = {"gx": lax.rem(gx + counts[0] - 1, counts[0])}
    down = {"gx": lax.rem(gx + 1, counts[0])}
    left = {"gy": lax.rem(gy + counts[1] - 1, counts[1])}
    right = {"gy": lax.rem(gy + 1, counts[1])}
    mesh_ids = pl.DeviceIdType.MESH

    fetch = pltpu.make_async_copy(hess_ref, hess, local_sems.at[0])
    fetch.start()
    inner_rows, inner_cols = pl.ds(reach, span_rows), pl.ds(reach, span_cols)
    home = pltpu.make_async_copy(tangent_ref, ext.at[inner_rows, inner_cols, :], local_sems.at[1])
    home.start()

    barrier = pltpu.get_barrier_semaphore()
    for neighbour in (up, down, left, right):
        pl.semaphore_signal(barrier, inc=1, device_id=neighbour, device_id_type=mesh_ids)
    pl.semaphore_wait(barrier, 4)

    first, last = pl.ds(0, reach), pl.ds(reach + span_rows, reach)
    first_cols, last_cols = pl.ds(0, reach), pl.ds(reach + span_cols, reach)
    chunks = depth // LANES
    lanes = [pl.ds(c * LANES, LANES) for c in range(chunks)]

    def remote(source, target, send_sem, recv_sem, device):
        return pltpu.make_async_remote_copy(
            src_ref=source, dst_ref=target, send_sem=send_sem, recv_sem=recv_sem,
            device_id=device, device_id_type=mesh_ids)

    head_rows, tail_rows = pl.ds(0, reach), pl.ds(span_rows - reach, reach)
    head_cols, tail_cols = pl.ds(0, reach), pl.ds(span_cols - reach, reach)
    copies = {}
    for c in range(chunks):
        z = lanes[c]
        every_row, every_col = pl.ds(0, span_rows), pl.ds(0, span_cols)
        plan = [
            (tangent_ref.at[tail_rows, every_col, z], ext.at[first, inner_cols, z], down),
            (tangent_ref.at[head_rows, every_col, z], ext.at[last, inner_cols, z], up),
            (tangent_ref.at[every_row, tail_cols, z], ext.at[inner_rows, first_cols, z], right),
            (tangent_ref.at[every_row, head_cols, z], ext.at[inner_rows, last_cols, z], left),
        ]
        near_last, near_first = pl.ds(span_cols, reach), pl.ds(reach, reach)
        for rows_at in (first, last):
            plan.append((ext.at[rows_at, near_last, z], ext.at[rows_at, first_cols, z], right))
            plan.append((ext.at[rows_at, near_first, z], ext.at[rows_at, last_cols, z], left))
        for kind, (source, target, device) in enumerate(plan):
            copies[kind, c] = remote(source, target, send_sems.at[kind, c], recv_sems.at[kind, c], device)
    for c in range(chunks):
        for kind in range(4):
            copies[kind, c].start()

    def relay(c):
        for kind in (0, 1):
            copies[kind, c].wait_recv()
        for kind in (4, 5, 6, 7):
            copies[kind, c].start()

    rows, cols = rows_ref[...], cols_ref[...]
    build_forward(sizes, rows, cols, by_row, by_col, fwd_high, fwd_low)
    home.wait()

    halves = max(1, depth // 256)
    half = depth // halves
    per_half = chunks // halves
    edge = reach * ext_cols

    def prepare(h, start, count):
        z = pl.ds(h * half, half)
        block = ext[pl.ds(start, count), :, z].reshape(count * ext_cols, half)
        at = pl.ds(start * ext_cols, count * ext_cols)
        high[at, z], low[at, z] = split(block)

    def lateral(h, ranges, fresh):
        z = pl.ds(h * half, half)

        def body(a, carry):
            part = pl.ds(pl.multiple_of(a * own, own), own)
            total = None if fresh else acc[part, z]
            for start, count in ranges:
                at = pl.ds(start, count)
                lead = fwd_high[part, at]
                piece = (dot(lead, high[at, z]) + dot(lead, low[at, z])
                         + dot(fwd_low[part, at], high[at, z]))
                total = piece if total is None else total + piece
            acc[part, z] = total
            return carry

        lax.fori_loop(0, DENSITIES, body, 0)

    def middle(h):
        for c in range(h * per_half, (h + 1) * per_half):
            copies[2, c].wait_recv()
            copies[3, c].wait_recv()
        prepare(h, reach, span_rows)
        lateral(h, [(edge, span_rows * ext_cols)], True)

    def edges(h):
        for c in range(h * per_half, (h + 1) * per_half):
            for kind in (4, 5, 6, 7):
                copies[kind, c].wait_recv()
        prepare(h, 0, reach)
        prepare(h, reach + span_rows, reach)
        lateral(h, [(0, edge), (edge + span_rows * ext_cols, edge)], False)

    build_bands(depth_ref[...].astype(jnp.float32), bands)
    relayed = 0
    for h in range(halves):
        middle(h)
        relay(relayed)
        relayed += 1
    build_backward(sizes, rows, cols, by_row_t, by_col_t, bwd_high, bwd_low)
    for h in range(halves):
        while relayed < min(chunks, (h + 1) * per_half + 1):
            relay(relayed)
            relayed += 1
        edges(h)

    def along_depth(a, carry):
        part = pl.ds(pl.multiple_of(a * own, own), own)
        acc[part, :] = dot(acc[part, :].astype(jnp.bfloat16), bands[a])
        return carry

    lax.fori_loop(0, DENSITIES, along_depth, 0)
    fetch.wait()

    def gradient(a, carry):
        part = pl.ds(pl.multiple_of(a * own, own), own)
        step = 16

        def piece(i, inner):
            at = pl.ds(pl.multiple_of(i * step, step), step)
            total = None
            for b in range(DENSITIES):
                there = pl.ds(pl.multiple_of(b * own + i * step, step), step)
                term = hess[a, b, at, :].astype(jnp.float32) * acc[there, :]
                total = term if total is None else total + term
            lowered[at, :] = total.astype(jnp.bfloat16)
            return inner

        lax.fori_loop(0, own // step, piece, 0)
        back = lax.dot_general(lowered[...], bands[a], (((1,), (1,)), ((), ())),
                               preferred_element_type=jnp.float32)
        back_high[part, :], back_low[part, :] = split(back)
        return carry

    lax.fori_loop(0, DENSITIES, gradient, 0)

    def contribute(h, start, count):
        z = pl.ds(h * half, half)
        at = pl.ds(start * ext_cols, count * ext_cols)
        lead = bwd_high[at, :]
        flat = dot(lead, back_high[:, z]) + dot(lead, back_low[:, z]) + dot(bwd_low[at, :], back_high[:, z])
        spread[pl.ds(start, count), :, z] = flat.reshape(count, ext_cols, half)

    returns = {}
    for h in range(halves):
        z = pl.ds(h * half, half)
        plan = []
        for rows_at in (first, last, inner_rows):
            plan.append((spread.at[rows_at, last_cols, z], from_left.at[rows_at, :, z], right))
            plan.append((spread.at[rows_at, first_cols, z], from_right.at[rows_at, :, z], left))
        plan.append((spread.at[first, inner_cols, z], from_down.at[:, :, z], up))
        plan.append((spread.at[last, inner_cols, z], from_up.at[:, :, z], down))
        for kind, (source, target, device) in enumerate(plan):
            returns[kind, h] = remote(source, target, back_send_sems.at[kind, h], back_recv_sems.at[kind, h], device)

    for h in range(halves):
        contribute(h, 0, reach)
        for kind in (0, 1):
            returns[kind, h].start()
        contribute(h, reach + span_rows, reach)
        for kind in (2, 3):
            returns[kind, h].start()

    def strips(h):
        z = pl.ds(h * half, half)
        for kind, rows_at, strip in ((0, first, 6), (2, last, 7)):
            returns[kind, h].wait_recv()
            returns[kind + 1, h].wait_recv()
            near = pl.ds(reach, reach)
            spread[rows_at, near, z] = spread[rows_at, near, z] + from_left[rows_at, :, z]
            far = pl.ds(span_cols, reach)
            spread[rows_at, far, z] = spread[rows_at, far, z] + from_right[rows_at, :, z]
            returns[strip, h].start()

    for h in range(halves):
        strips(h)
    for h in range(halves):
        for start in range(reach, reach + span_rows, reach):
            contribute(h, start, reach)
        for kind in (4, 5):
            returns[kind, h].start()
    for h in range(halves):
        z = pl.ds(h * half, half)
        for kind in (4, 5):
            returns[kind, h].wait_recv()
        out_ref[:, :, z] = spread[inner_rows, inner_cols, z]
        out_ref[:, head_cols, z] = out_ref[:, head_cols, z] + from_left[inner_rows, :, z]
        out_ref[:, tail_cols, z] = out_ref[:, tail_cols, z] + from_right[inner_rows, :, z]
        for kind in (6, 7):
            returns[kind, h].wait_recv()
        out_ref[head_rows, :, z] = out_ref[head_rows, :, z] + from_up[:, :, z]
        out_ref[tail_rows, :, z] = out_ref[tail_rows, :, z] + from_down[:, :, z]
    for copy in list(copies.values()) + list(returns.values()):
        copy.wait_send()


def per_device(tangent, hessian, kernel_rows, kernel_cols, kernel_depth):
    span_rows, span_cols, depth = tangent.shape
    reach = RADIUS
    ext_rows, ext_cols = span_rows + 2 * reach, span_cols + 2 * reach
    sizes = (span_rows, span_cols, ext_rows, ext_cols)
    counts = (lax.axis_size("gx"), lax.axis_size("gy"))
    own, wide = span_rows * span_cols, ext_rows * ext_cols
    chunks, halves = depth // LANES, max(1, depth // 256)
    full = pl.BlockSpec(memory_space=pltpu.VMEM)
    anywhere = pl.BlockSpec(memory_space=pl.ANY)
    bf16, f32 = jnp.bfloat16, jnp.float32
    return pl.pallas_call(
        lambda *refs: compute(sizes, counts, *refs),
        out_shape=jax.ShapeDtypeStruct((span_rows, span_cols, depth), f32),
        in_specs=[anywhere, anywhere, full, full, full],
        out_specs=full,
        scratch_shapes=[
            pltpu.VMEM((ext_rows, ext_cols, depth), f32),
            pltpu.VMEM((wide, depth), bf16),
            pltpu.VMEM((wide, depth), bf16),
            pltpu.VMEM((span_rows, wide), f32),
            pltpu.VMEM((span_cols, wide), f32),
            pltpu.VMEM((ext_rows, DENSITIES * own), f32),
            pltpu.VMEM((ext_cols, DENSITIES * own), f32),
            pltpu.VMEM((DENSITIES * own, wide), bf16),
            pltpu.VMEM((DENSITIES * own, wide), bf16),
            pltpu.VMEM((wide, DENSITIES * own), bf16),
            pltpu.VMEM((wide, DENSITIES * own), bf16),
            pltpu.VMEM((DENSITIES, depth, depth), bf16),
            pltpu.VMEM((DENSITIES, DENSITIES, own, depth), bf16),
            pltpu.VMEM((own, depth), bf16),
            pltpu.VMEM((DENSITIES * own, depth), f32),
            pltpu.VMEM((DENSITIES * own, depth), bf16),
            pltpu.VMEM((DENSITIES * own, depth), bf16),
            pltpu.VMEM((ext_rows, ext_cols, depth), f32),
            pltpu.VMEM((ext_rows, reach, depth), f32),
            pltpu.VMEM((ext_rows, reach, depth), f32),
            pltpu.VMEM((reach, span_cols, depth), f32),
            pltpu.VMEM((reach, span_cols, depth), f32),
            pltpu.SemaphoreType.DMA((2,)),
            pltpu.SemaphoreType.DMA((8, chunks)),
            pltpu.SemaphoreType.DMA((8, chunks)),
            pltpu.SemaphoreType.DMA((8, halves)),
            pltpu.SemaphoreType.DMA((8, halves)),
        ],
        compiler_params=pltpu.CompilerParams(
            vmem_limit_bytes=60 << 20, collective_id=0, has_side_effects=True),
    )(tangent, hessian.reshape(DENSITIES, DENSITIES, own, depth), kernel_rows, kernel_cols, kernel_depth)


def solution(mesh):
    return jax.shard_map(
        per_device,
        mesh=mesh,
        in_specs=(P("gx", "gy", None), P(None, None, "gx", "gy", None), P(), P(), P()),
        out_specs=P("gx", "gy", None),
        check_vma=False,
    )
```

```python
import jax
import jax.numpy as jnp
from jax import lax
from jax.experimental import pallas as pl
from jax.experimental.pallas import tpu as pltpu
from jax.sharding import PartitionSpec as P

RADIUS = 8
DENSITIES = 5
TAPS = 2 * RADIUS + 1
LANES = 128


def split(value):
    high = value.astype(jnp.bfloat16)
    low = (value - high.astype(jnp.float32)).astype(jnp.bfloat16)
    return high, low


def dot(left, right):
    return jnp.dot(left, right, preferred_element_type=jnp.float32)


def picked(taps, index):
    total = jnp.zeros(index.shape, jnp.float32)
    for tap in range(TAPS):
        weight = jnp.broadcast_to(taps[:, tap : tap + 1], index.shape)
        total = jnp.where(index == tap, weight, total)
    return total


def build_forward(sizes, rows, cols, by_row, by_col, high_ref, low_ref):
    span_rows, span_cols, ext_rows, ext_cols = sizes
    wide = ext_rows * ext_cols
    lane = lax.broadcasted_iota(jnp.int32, (span_rows, wide), 1)
    row_index = lane // ext_cols - lax.broadcasted_iota(jnp.int32, (span_rows, wide), 0)
    lane = lax.broadcasted_iota(jnp.int32, (span_cols, wide), 1)
    col_index = lane % ext_cols - lax.broadcasted_iota(jnp.int32, (span_cols, wide), 0)
    for a in range(DENSITIES):
        by_row[...] = picked(rows[a : a + 1], row_index)
        by_col[...] = picked(cols[a : a + 1], col_index)

        def body(r, carry):
            high, low = split(by_row[pl.ds(r, 1), :] * by_col[...])
            start = pl.multiple_of((a * span_rows + r) * span_cols, span_cols)
            high_ref[pl.ds(start, span_cols), :] = high
            low_ref[pl.ds(start, span_cols), :] = low
            return carry

        lax.fori_loop(0, span_rows, body, 0)


def build_backward(sizes, rows, cols, by_row, by_col, high_ref, low_ref):
    span_rows, span_cols, ext_rows, ext_cols = sizes
    own = span_rows * span_cols
    lane = lax.broadcasted_iota(jnp.int32, (ext_rows, own), 1)
    row_index = lax.broadcasted_iota(jnp.int32, (ext_rows, own), 0) - lane // span_cols
    lane = lax.broadcasted_iota(jnp.int32, (ext_cols, own), 1)
    col_index = lax.broadcasted_iota(jnp.int32, (ext_cols, own), 0) - lane % span_cols
    for a in range(DENSITIES):
        by_row[:, a * own : (a + 1) * own] = picked(rows[a : a + 1], row_index)
        by_col[:, a * own : (a + 1) * own] = picked(cols[a : a + 1], col_index)

    def body(r, carry):
        high, low = split(by_row[pl.ds(r, 1), :] * by_col[...])
        start = pl.multiple_of(r * ext_cols, ext_cols)
        high_ref[pl.ds(start, ext_cols), :] = high
        low_ref[pl.ds(start, ext_cols), :] = low
        return carry

    lax.fori_loop(0, ext_rows, body, 0)


def build_bands(depth_taps, band_ref):
    depth = band_ref.shape[1]
    blocks = depth // LANES
    shape = (LANES, LANES)
    index = lax.broadcasted_iota(jnp.int32, shape, 0) - lax.broadcasted_iota(jnp.int32, shape, 1) + RADIUS
    for a in range(DENSITIES):
        taps = depth_taps[a : a + 1]
        same = picked(taps, index).astype(jnp.bfloat16)
        after = picked(taps, index - LANES).astype(jnp.bfloat16)
        before = picked(taps, index + LANES).astype(jnp.bfloat16)
        for p in range(blocks):
            for q in range(blocks):
                block = {0: same, 1: after, -1: before}.get(q - p, jnp.zeros(shape, jnp.bfloat16))
                band_ref[a, p * LANES : (p + 1) * LANES, q * LANES : (q + 1) * LANES] = block


def compute(sizes, counts, tangent_ref, hess_ref, rows_ref, cols_ref, depth_ref, out_ref,
            ext, high, low, by_row, by_col, by_row_t, by_col_t, fwd_high, fwd_low, bwd_high, bwd_low,
            bands, hess, lowered, acc, dens, back_high, back_low, spread, from_left, from_right,
            from_up, from_down, local_sems, send_sems, recv_sems, back_send_sems, back_recv_sems):
    span_rows, span_cols, ext_rows, ext_cols = sizes
    depth = acc.shape[1]
    reach = RADIUS
    own, wide = span_rows * span_cols, ext_rows * ext_cols
    gx, gy = lax.axis_index("gx"), lax.axis_index("gy")
    up = {"gx": lax.rem(gx + counts[0] - 1, counts[0])}
    down = {"gx": lax.rem(gx + 1, counts[0])}
    left = {"gy": lax.rem(gy + counts[1] - 1, counts[1])}
    right = {"gy": lax.rem(gy + 1, counts[1])}
    mesh_ids = pl.DeviceIdType.MESH

    fetch = pltpu.make_async_copy(hess_ref, hess, local_sems.at[0])
    fetch.start()
    inner_rows, inner_cols = pl.ds(reach, span_rows), pl.ds(reach, span_cols)
    home = pltpu.make_async_copy(tangent_ref, ext.at[inner_rows, inner_cols, :], local_sems.at[1])
    home.start()

    barrier = pltpu.get_barrier_semaphore()
    for neighbour in (up, down, left, right):
        pl.semaphore_signal(barrier, inc=1, device_id=neighbour, device_id_type=mesh_ids)
    rows, cols = rows_ref[...], cols_ref[...]
    build_forward(sizes, rows, cols, by_row, by_col, fwd_high, fwd_low)
    build_bands(depth_ref[...].astype(jnp.float32), bands)
    build_backward(sizes, rows, cols, by_row_t, by_col_t, bwd_high, bwd_low)
    pl.semaphore_wait(barrier, 4)

    first, last = pl.ds(0, reach), pl.ds(reach + span_rows, reach)
    first_cols, last_cols = pl.ds(0, reach), pl.ds(reach + span_cols, reach)
    chunks = depth // LANES
    lanes = [pl.ds(c * LANES, LANES) for c in range(chunks)]

    def remote(source, target, send_sem, recv_sem, device):
        return pltpu.make_async_remote_copy(
            src_ref=source, dst_ref=target, send_sem=send_sem, recv_sem=recv_sem,
            device_id=device, device_id_type=mesh_ids)

    head_rows, tail_rows = pl.ds(0, reach), pl.ds(span_rows - reach, reach)
    head_cols, tail_cols = pl.ds(0, reach), pl.ds(span_cols - reach, reach)
    copies = {}
    for c in range(chunks):
        z = lanes[c]
        every_row, every_col = pl.ds(0, span_rows), pl.ds(0, span_cols)
        plan = [
            (tangent_ref.at[tail_rows, every_col, z], ext.at[first, inner_cols, z], down),
            (tangent_ref.at[head_rows, every_col, z], ext.at[last, inner_cols, z], up),
            (tangent_ref.at[every_row, tail_cols, z], ext.at[inner_rows, first_cols, z], right),
            (tangent_ref.at[every_row, head_cols, z], ext.at[inner_rows, last_cols, z], left),
        ]
        near_last, near_first = pl.ds(span_cols, reach), pl.ds(reach, reach)
        for rows_at in (first, last):
            plan.append((ext.at[rows_at, near_last, z], ext.at[rows_at, first_cols, z], right))
            plan.append((ext.at[rows_at, near_first, z], ext.at[rows_at, last_cols, z], left))
        for kind, (source, target, device) in enumerate(plan):
            copies[kind, c] = remote(source, target, send_sems.at[kind, c], recv_sems.at[kind, c], device)
    for c in range(chunks):
        for kind in range(4):
            copies[kind, c].start()

    def relay(c):
        for kind in (0, 1):
            copies[kind, c].wait_recv()
        for kind in (4, 5, 6, 7):
            copies[kind, c].start()

    home.wait()

    halves = max(1, depth // 256)
    half = depth // halves
    per_half = chunks // halves
    edge = reach * ext_cols

    def prepare(z, start, count):
        block = ext[pl.ds(start, count), :, z].reshape(count * ext_cols, z.size)
        at = pl.ds(start * ext_cols, count * ext_cols)
        high[at, z], low[at, z] = split(block)

    def lateral(z, ranges, fresh):
        def body(a, carry):
            part = pl.ds(pl.multiple_of(a * own, own), own)
            total = None if fresh else acc[part, z]
            for start, count in ranges:
                at = pl.ds(start, count)
                lead = fwd_high[part, at]
                piece = (dot(lead, high[at, z]) + dot(lead, low[at, z])
                         + dot(fwd_low[part, at], high[at, z]))
                total = piece if total is None else total + piece
            acc[part, z] = total
            return carry

        lax.fori_loop(0, DENSITIES, body, 0)

    def middle(h):
        for c in range(h * per_half, (h + 1) * per_half):
            copies[2, c].wait_recv()
            copies[3, c].wait_recv()
        z = pl.ds(h * half, half)
        prepare(z, reach, span_rows)
        lateral(z, [(edge, span_rows * ext_cols)], True)

    def edges(begin, end):
        for c in range(begin, end):
            for kind in (4, 5, 6, 7):
                copies[kind, c].wait_recv()
        z = pl.ds(begin * LANES, (end - begin) * LANES)
        prepare(z, 0, reach)
        prepare(z, reach + span_rows, reach)
        lateral(z, [(0, edge), (edge + span_rows * ext_cols, edge)], False)

    def along_depth(source, target):
        def body(a, carry):
            part = pl.ds(pl.multiple_of(a * own, own), own)
            dens[part, target] = dot(acc[part, source].astype(jnp.bfloat16), bands[a, source, target])
            return carry

        lax.fori_loop(0, DENSITIES, body, 0)

    def gradient(middle_lanes, source, target):
        def body(a, carry):
            part = pl.ds(pl.multiple_of(a * own, own), own)
            step = 16

            def piece(i, inner):
                at = pl.ds(pl.multiple_of(i * step, step), step)
                total = None
                for b in range(DENSITIES):
                    there = pl.ds(pl.multiple_of(b * own + i * step, step), step)
                    term = hess[a, b, at, middle_lanes].astype(jnp.float32) * dens[there, middle_lanes]
                    total = term if total is None else total + term
                into = pl.ds(pl.multiple_of(a * own + i * step, step), step)
                lowered[into, middle_lanes] = total.astype(jnp.bfloat16)
                return inner

            lax.fori_loop(0, own // step, piece, 0)
            back = lax.dot_general(lowered[part, source], bands[a, target, source],
                                   (((1,), (1,)), ((), ())), preferred_element_type=jnp.float32)
            back_high[part, target], back_low[part, target] = split(back)
            return carry

        lax.fori_loop(0, DENSITIES, body, 0)

    def contribute(h, start, count):
        z = pl.ds(h * half, half)
        at = pl.ds(start * ext_cols, count * ext_cols)
        lead = bwd_high[at, :]
        flat = dot(lead, back_high[:, z]) + dot(lead, back_low[:, z]) + dot(bwd_low[at, :], back_high[:, z])
        spread[pl.ds(start, count), :, z] = flat.reshape(count, ext_cols, half)

    returns = {}
    for h in range(halves):
        z = pl.ds(h * half, half)
        plan = []
        for rows_at in (first, last, inner_rows):
            plan.append((spread.at[rows_at, last_cols, z], from_left.at[rows_at, :, z], right))
            plan.append((spread.at[rows_at, first_cols, z], from_right.at[rows_at, :, z], left))
        plan.append((spread.at[first, inner_cols, z], from_down.at[:, :, z], up))
        plan.append((spread.at[last, inner_cols, z], from_up.at[:, :, z], down))
        for kind, (source, target, device) in enumerate(plan):
            returns[kind, h] = remote(source, target, back_send_sems.at[kind, h], back_recv_sems.at[kind, h], device)

    def strips(h):
        z = pl.ds(h * half, half)
        for kind, rows_at, strip in ((0, first, 6), (2, last, 7)):
            returns[kind, h].wait_recv()
            returns[kind + 1, h].wait_recv()
            near = pl.ds(reach, reach)
            spread[rows_at, near, z] = spread[rows_at, near, z] + from_left[rows_at, :, z]
            far = pl.ds(span_cols, reach)
            spread[rows_at, far, z] = spread[rows_at, far, z] + from_right[rows_at, :, z]
            returns[strip, h].start()

    def corners(h):
        contribute(h, 0, reach)
        for kind in (0, 1):
            returns[kind, h].start()
        contribute(h, reach + span_rows, reach)
        for kind in (2, 3):
            returns[kind, h].start()

    def sides(h):
        for start in range(reach, reach + span_rows, reach):
            contribute(h, start, reach)
        for kind in (4, 5):
            returns[kind, h].start()

    relayed = 0
    ready = 0
    for h in range(halves):
        middle(h)
        if relayed < chunks:
            relay(relayed)
            relayed += 1
    for h in range(halves):
        need = min(chunks, (h + 1) * per_half + 1)
        while ready < need:
            stop = min(need, ready + per_half)
            while relayed < stop:
                relay(relayed)
                relayed += 1
            edges(ready, stop)
            ready = stop
        if relayed < chunks:
            relay(relayed)
            relayed += 1
        begin = h * half
        source = pl.ds(max(0, begin - LANES), need * LANES - max(0, begin - LANES))
        fresh = pl.ds(begin, need * LANES - begin)
        along_depth(source, fresh)
        if h == 0:
            fetch.wait()
        else:
            strips(h - 1)
        gradient(fresh, source, pl.ds(begin, half))
        corners(h)
        if h > 0:
            sides(h - 1)
    strips(halves - 1)
    sides(halves - 1)
    for h in range(halves):
        z = pl.ds(h * half, half)
        for kind in (4, 5):
            returns[kind, h].wait_recv()
        out_ref[:, :, z] = spread[inner_rows, inner_cols, z]
        out_ref[:, head_cols, z] = out_ref[:, head_cols, z] + from_left[inner_rows, :, z]
        out_ref[:, tail_cols, z] = out_ref[:, tail_cols, z] + from_right[inner_rows, :, z]
        for kind in (6, 7):
            returns[kind, h].wait_recv()
        out_ref[head_rows, :, z] = out_ref[head_rows, :, z] + from_up[:, :, z]
        out_ref[tail_rows, :, z] = out_ref[tail_rows, :, z] + from_down[:, :, z]
    for copy in list(copies.values()) + list(returns.values()):
        copy.wait_send()


def per_device(tangent, hessian, kernel_rows, kernel_cols, kernel_depth):
    span_rows, span_cols, depth = tangent.shape
    reach = RADIUS
    ext_rows, ext_cols = span_rows + 2 * reach, span_cols + 2 * reach
    sizes = (span_rows, span_cols, ext_rows, ext_cols)
    counts = (lax.axis_size("gx"), lax.axis_size("gy"))
    own, wide = span_rows * span_cols, ext_rows * ext_cols
    chunks, halves = depth // LANES, max(1, depth // 256)
    full = pl.BlockSpec(memory_space=pltpu.VMEM)
    anywhere = pl.BlockSpec(memory_space=pl.ANY)
    bf16, f32 = jnp.bfloat16, jnp.float32
    return pl.pallas_call(
        lambda *refs: compute(sizes, counts, *refs),
        out_shape=jax.ShapeDtypeStruct((span_rows, span_cols, depth), f32),
        in_specs=[anywhere, anywhere, full, full, full],
        out_specs=full,
        scratch_shapes=[
            pltpu.VMEM((ext_rows, ext_cols, depth), f32),
            pltpu.VMEM((wide, depth), bf16),
            pltpu.VMEM((wide, depth), bf16),
            pltpu.VMEM((span_rows, wide), f32),
            pltpu.VMEM((span_cols, wide), f32),
            pltpu.VMEM((ext_rows, DENSITIES * own), f32),
            pltpu.VMEM((ext_cols, DENSITIES * own), f32),
            pltpu.VMEM((DENSITIES * own, wide), bf16),
            pltpu.VMEM((DENSITIES * own, wide), bf16),
            pltpu.VMEM((wide, DENSITIES * own), bf16),
            pltpu.VMEM((wide, DENSITIES * own), bf16),
            pltpu.VMEM((DENSITIES, depth, depth), bf16),
            pltpu.VMEM((DENSITIES, DENSITIES, own, depth), bf16),
            pltpu.VMEM((DENSITIES * own, depth), bf16),
            pltpu.VMEM((DENSITIES * own, depth), f32),
            pltpu.VMEM((DENSITIES * own, depth), f32),
            pltpu.VMEM((DENSITIES * own, depth), bf16),
            pltpu.VMEM((DENSITIES * own, depth), bf16),
            pltpu.VMEM((ext_rows, ext_cols, depth), f32),
            pltpu.VMEM((ext_rows, reach, depth), f32),
            pltpu.VMEM((ext_rows, reach, depth), f32),
            pltpu.VMEM((reach, span_cols, depth), f32),
            pltpu.VMEM((reach, span_cols, depth), f32),
            pltpu.SemaphoreType.DMA((2,)),
            pltpu.SemaphoreType.DMA((8, chunks)),
            pltpu.SemaphoreType.DMA((8, chunks)),
            pltpu.SemaphoreType.DMA((8, halves)),
            pltpu.SemaphoreType.DMA((8, halves)),
        ],
        compiler_params=pltpu.CompilerParams(
            vmem_limit_bytes=60 << 20, collective_id=0, has_side_effects=True),
    )(tangent, hessian.reshape(DENSITIES, DENSITIES, own, depth), kernel_rows, kernel_cols, kernel_depth)


def solution(mesh):
    return jax.shard_map(
        per_device,
        mesh=mesh,
        in_specs=(P("gx", "gy", None), P(None, None, "gx", "gy", None), P(), P(), P()),
        out_specs=P("gx", "gy", None),
        check_vma=False,
    )
```

```python
import jax
import jax.numpy as jnp
from jax import lax
from jax.experimental import pallas as pl
from jax.experimental.pallas import tpu as pltpu
from jax.sharding import PartitionSpec as P

RADIUS = 8
DENSITIES = 5
TAPS = 2 * RADIUS + 1
LANES = 128


def split(value):
    high = value.astype(jnp.bfloat16)
    low = (value - high.astype(jnp.float32)).astype(jnp.bfloat16)
    return high, low


def dot(left, right):
    return jnp.dot(left, right, preferred_element_type=jnp.float32)


def picked(taps, index):
    total = jnp.zeros(index.shape, jnp.float32)
    for tap in range(TAPS):
        weight = jnp.broadcast_to(taps[:, tap : tap + 1], index.shape)
        total = jnp.where(index == tap, weight, total)
    return total


def build_forward(sizes, pieces, rows, cols, by_row, by_col, packed_ref):
    span_rows, span_cols, ext_rows, ext_cols = sizes
    wide = ext_rows * ext_cols
    lane = lax.broadcasted_iota(jnp.int32, (span_rows, wide), 1)
    row_index = lane // ext_cols - lax.broadcasted_iota(jnp.int32, (span_rows, wide), 0)
    lane = lax.broadcasted_iota(jnp.int32, (span_cols, wide), 1)
    col_index = lane % ext_cols - lax.broadcasted_iota(jnp.int32, (span_cols, wide), 0)
    for a in range(DENSITIES):
        by_row[...] = picked(rows[a : a + 1], row_index)
        by_col[...] = picked(cols[a : a + 1], col_index)

        def body(r, carry):
            high, low = split(by_row[pl.ds(r, 1), :] * by_col[...])
            at = pl.ds(pl.multiple_of((a * span_rows + r) * span_cols, span_cols), span_cols)
            for offset, length, begin in pieces:
                for copy, value in enumerate((high, high, low)):
                    start = 3 * offset[0] + copy * offset[1] + offset[2]
                    packed_ref[at, start : start + length] = value[:, begin : begin + length]
            return carry

        lax.fori_loop(0, span_rows, body, 0)


def build_backward(sizes, rows, cols, by_row, by_col, high_ref, low_ref):
    span_rows, span_cols, ext_rows, ext_cols = sizes
    own = span_rows * span_cols
    lane = lax.broadcasted_iota(jnp.int32, (ext_rows, own), 1)
    row_index = lax.broadcasted_iota(jnp.int32, (ext_rows, own), 0) - lane // span_cols
    lane = lax.broadcasted_iota(jnp.int32, (ext_cols, own), 1)
    col_index = lax.broadcasted_iota(jnp.int32, (ext_cols, own), 0) - lane % span_cols
    for a in range(DENSITIES):
        by_row[:, a * own : (a + 1) * own] = picked(rows[a : a + 1], row_index)
        by_col[:, a * own : (a + 1) * own] = picked(cols[a : a + 1], col_index)

    def body(r, carry):
        high, low = split(by_row[pl.ds(r, 1), :] * by_col[...])
        start = pl.multiple_of(r * ext_cols, ext_cols)
        high_ref[pl.ds(start, ext_cols), :] = high
        low_ref[pl.ds(start, ext_cols), :] = low
        return carry

    lax.fori_loop(0, ext_rows, body, 0)


def build_bands(depth_taps, band_ref):
    depth = band_ref.shape[1]
    blocks = depth // LANES
    shape = (LANES, LANES)
    index = lax.broadcasted_iota(jnp.int32, shape, 0) - lax.broadcasted_iota(jnp.int32, shape, 1) + RADIUS
    for a in range(DENSITIES):
        taps = depth_taps[a : a + 1]
        same = picked(taps, index).astype(jnp.bfloat16)
        after = picked(taps, index - LANES).astype(jnp.bfloat16)
        before = picked(taps, index + LANES).astype(jnp.bfloat16)
        for p in range(blocks):
            for q in range(blocks):
                block = {0: same, 1: after, -1: before}.get(q - p, jnp.zeros(shape, jnp.bfloat16))
                band_ref[a, p * LANES : (p + 1) * LANES, q * LANES : (q + 1) * LANES] = block


def compute(sizes, counts, tangent_ref, hess_ref, rows_ref, cols_ref, depth_ref, out_ref,
            ext, parts, by_row, by_col, by_row_t, by_col_t, fwd, bwd_high, bwd_low,
            bands, hess, lowered, acc, dens, back_high, back_low, spread, from_left, from_right,
            from_up, from_down, local_sems, send_sems, recv_sems, back_send_sems, back_recv_sems):
    span_rows, span_cols, ext_rows, ext_cols = sizes
    depth = acc.shape[1]
    reach = RADIUS
    own, wide = span_rows * span_cols, ext_rows * ext_cols
    edge, inner = reach * ext_cols, span_rows * ext_cols
    pieces = (((0, inner, 0), inner, edge), ((inner, 2 * edge, 0), edge, 0),
              ((inner, 2 * edge, edge), edge, edge + inner))
    gx, gy = lax.axis_index("gx"), lax.axis_index("gy")
    up = {"gx": lax.rem(gx + counts[0] - 1, counts[0])}
    down = {"gx": lax.rem(gx + 1, counts[0])}
    left = {"gy": lax.rem(gy + counts[1] - 1, counts[1])}
    right = {"gy": lax.rem(gy + 1, counts[1])}
    mesh_ids = pl.DeviceIdType.MESH

    fetch = pltpu.make_async_copy(hess_ref, hess, local_sems.at[0])
    fetch.start()
    inner_rows, inner_cols = pl.ds(reach, span_rows), pl.ds(reach, span_cols)
    home = pltpu.make_async_copy(tangent_ref, ext.at[inner_rows, inner_cols, :], local_sems.at[1])
    home.start()

    barrier = pltpu.get_barrier_semaphore()
    for neighbour in (up, down, left, right):
        pl.semaphore_signal(barrier, inc=1, device_id=neighbour, device_id_type=mesh_ids)
    pl.semaphore_wait(barrier, 4)

    first, last = pl.ds(0, reach), pl.ds(reach + span_rows, reach)
    first_cols, last_cols = pl.ds(0, reach), pl.ds(reach + span_cols, reach)
    chunks = depth // LANES
    lanes = [pl.ds(c * LANES, LANES) for c in range(chunks)]

    def remote(source, target, send_sem, recv_sem, device):
        return pltpu.make_async_remote_copy(
            src_ref=source, dst_ref=target, send_sem=send_sem, recv_sem=recv_sem,
            device_id=device, device_id_type=mesh_ids)

    head_rows, tail_rows = pl.ds(0, reach), pl.ds(span_rows - reach, reach)
    head_cols, tail_cols = pl.ds(0, reach), pl.ds(span_cols - reach, reach)
    copies = {}
    for c in range(chunks):
        z = lanes[c]
        every_row, every_col = pl.ds(0, span_rows), pl.ds(0, span_cols)
        plan = [
            (tangent_ref.at[tail_rows, every_col, z], ext.at[first, inner_cols, z], down),
            (tangent_ref.at[head_rows, every_col, z], ext.at[last, inner_cols, z], up),
            (tangent_ref.at[every_row, tail_cols, z], ext.at[inner_rows, first_cols, z], right),
            (tangent_ref.at[every_row, head_cols, z], ext.at[inner_rows, last_cols, z], left),
        ]
        near_last, near_first = pl.ds(span_cols, reach), pl.ds(reach, reach)
        for rows_at in (first, last):
            plan.append((ext.at[rows_at, near_last, z], ext.at[rows_at, first_cols, z], right))
            plan.append((ext.at[rows_at, near_first, z], ext.at[rows_at, last_cols, z], left))
        for kind, (source, target, device) in enumerate(plan):
            copies[kind, c] = remote(source, target, send_sems.at[kind, c], recv_sems.at[kind, c], device)
    for c in range(chunks):
        for kind in range(4):
            copies[kind, c].start()

    def relay(c):
        for kind in (0, 1):
            copies[kind, c].wait_recv()
        for kind in (4, 5, 6, 7):
            copies[kind, c].start()

    rows, cols = rows_ref[...], cols_ref[...]
    build_forward(sizes, pieces, rows, cols, by_row, by_col, fwd)
    build_bands(depth_ref[...].astype(jnp.float32), bands)
    build_backward(sizes, rows, cols, by_row_t, by_col_t, bwd_high, bwd_low)
    home.wait()

    halves = max(1, depth // 256)
    half = depth // halves
    per_half = chunks // halves

    def prepare(z, piece):
        offset, length, begin = piece
        block = ext[pl.ds(begin // ext_cols, length // ext_cols), :, z].reshape(length, z.size)
        high, low = split(block)
        for copy, value in enumerate((high, low, high)):
            parts[pl.ds(3 * offset[0] + copy * offset[1] + offset[2], length), z] = value

    def lateral(z, start, length, fresh):
        def body(a, carry):
            part = pl.ds(pl.multiple_of(a * own, own), own)
            total = dot(fwd[part, pl.ds(start, length)], parts[pl.ds(start, length), z])
            acc[part, z] = total if fresh else acc[part, z] + total
            return carry

        lax.fori_loop(0, DENSITIES, body, 0)

    def middle(h):
        for c in range(h * per_half, (h + 1) * per_half):
            copies[2, c].wait_recv()
            copies[3, c].wait_recv()
        z = pl.ds(h * half, half)
        prepare(z, pieces[0])
        lateral(z, 0, 3 * inner, True)

    def edges(begin, end):
        for c in range(begin, end):
            for kind in (4, 5, 6, 7):
                copies[kind, c].wait_recv()
        z = pl.ds(begin * LANES, (end - begin) * LANES)
        prepare(z, pieces[1])
        prepare(z, pieces[2])
        lateral(z, 3 * inner, 6 * edge, False)

    def along_depth(source, target):
        def body(a, carry):
            part = pl.ds(pl.multiple_of(a * own, own), own)
            dens[part, target] = dot(acc[part, source].astype(jnp.bfloat16), bands[a, source, target])
            return carry

        lax.fori_loop(0, DENSITIES, body, 0)

    def gradient(middle_lanes, source, target):
        step = 16

        def piece(i, carry):
            at = pl.ds(pl.multiple_of(i * step, step), step)
            for lane in range(middle_lanes.start, middle_lanes.start + middle_lanes.size, LANES):
                z = pl.ds(lane, LANES)
                values = [dens[pl.ds(pl.multiple_of(b * own + i * step, step), step), z]
                          for b in range(DENSITIES)]
                for a in range(DENSITIES):
                    total = None
                    for b in range(DENSITIES):
                        term = hess[a, b, at, z].astype(jnp.float32) * values[b]
                        total = term if total is None else total + term
                    into = pl.ds(pl.multiple_of(a * own + i * step, step), step)
                    lowered[into, z] = total.astype(jnp.bfloat16)
            return carry

        lax.fori_loop(0, own // step, piece, 0)

        def body(a, carry):
            part = pl.ds(pl.multiple_of(a * own, own), own)
            back = lax.dot_general(lowered[part, source], bands[a, target, source],
                                   (((1,), (1,)), ((), ())), preferred_element_type=jnp.float32)
            back_high[part, target], back_low[part, target] = split(back)
            return carry

        lax.fori_loop(0, DENSITIES, body, 0)

    def contribute(h, start, count):
        z = pl.ds(h * half, half)
        at = pl.ds(start * ext_cols, count * ext_cols)
        lead = bwd_high[at, :]
        flat = dot(lead, back_high[:, z]) + dot(lead, back_low[:, z]) + dot(bwd_low[at, :], back_high[:, z])
        spread[pl.ds(start, count), :, z] = flat.reshape(count, ext_cols, half)

    returns = {}
    for h in range(halves):
        z = pl.ds(h * half, half)
        plan = []
        for rows_at in (first, last, inner_rows):
            plan.append((spread.at[rows_at, last_cols, z], from_left.at[rows_at, :, z], right))
            plan.append((spread.at[rows_at, first_cols, z], from_right.at[rows_at, :, z], left))
        plan.append((spread.at[first, inner_cols, z], from_down.at[:, :, z], up))
        plan.append((spread.at[last, inner_cols, z], from_up.at[:, :, z], down))
        for kind, (source, target, device) in enumerate(plan):
            returns[kind, h] = remote(source, target, back_send_sems.at[kind, h], back_recv_sems.at[kind, h], device)

    def strips(h):
        z = pl.ds(h * half, half)
        for kind, rows_at, strip in ((0, first, 6), (2, last, 7)):
            returns[kind, h].wait_recv()
            returns[kind + 1, h].wait_recv()
            near = pl.ds(reach, reach)
            spread[rows_at, near, z] = spread[rows_at, near, z] + from_left[rows_at, :, z]
            far = pl.ds(span_cols, reach)
            spread[rows_at, far, z] = spread[rows_at, far, z] + from_right[rows_at, :, z]
            returns[strip, h].start()

    def corners(h):
        contribute(h, 0, reach)
        for kind in (0, 1):
            returns[kind, h].start()
        contribute(h, reach + span_rows, reach)
        for kind in (2, 3):
            returns[kind, h].start()

    def sides(h):
        for start in range(reach, reach + span_rows, reach):
            contribute(h, start, reach)
        for kind in (4, 5):
            returns[kind, h].start()

    relayed = 0
    for h in range(halves):
        middle(h)
        if relayed < chunks:
            relay(relayed)
            relayed += 1
    while relayed < chunks:
        relay(relayed)
        relayed += 1
    for h in range(halves):
        edges(h * per_half, (h + 1) * per_half)
    every = pl.ds(0, depth)
    along_depth(every, every)
    fetch.wait()
    gradient(every, every, every)
    for h in range(halves):
        corners(h)
    for h in range(halves):
        strips(h)
    for h in range(halves):
        sides(h)
    for h in range(halves):
        z = pl.ds(h * half, half)
        for kind in (4, 5):
            returns[kind, h].wait_recv()
        out_ref[:, :, z] = spread[inner_rows, inner_cols, z]
        out_ref[:, head_cols, z] = out_ref[:, head_cols, z] + from_left[inner_rows, :, z]
        out_ref[:, tail_cols, z] = out_ref[:, tail_cols, z] + from_right[inner_rows, :, z]
        for kind in (6, 7):
            returns[kind, h].wait_recv()
        out_ref[head_rows, :, z] = out_ref[head_rows, :, z] + from_up[:, :, z]
        out_ref[tail_rows, :, z] = out_ref[tail_rows, :, z] + from_down[:, :, z]
    for copy in list(copies.values()) + list(returns.values()):
        copy.wait_send()


def per_device(tangent, hessian, kernel_rows, kernel_cols, kernel_depth):
    span_rows, span_cols, depth = tangent.shape
    reach = RADIUS
    ext_rows, ext_cols = span_rows + 2 * reach, span_cols + 2 * reach
    sizes = (span_rows, span_cols, ext_rows, ext_cols)
    counts = (lax.axis_size("gx"), lax.axis_size("gy"))
    own, wide = span_rows * span_cols, ext_rows * ext_cols
    chunks, halves = depth // LANES, max(1, depth // 256)
    full = pl.BlockSpec(memory_space=pltpu.VMEM)
    anywhere = pl.BlockSpec(memory_space=pl.ANY)
    bf16, f32 = jnp.bfloat16, jnp.float32
    return pl.pallas_call(
        lambda *refs: compute(sizes, counts, *refs),
        out_shape=jax.ShapeDtypeStruct((span_rows, span_cols, depth), f32),
        in_specs=[anywhere, anywhere, full, full, full],
        out_specs=full,
        scratch_shapes=[
            pltpu.VMEM((ext_rows, ext_cols, depth), f32),
            pltpu.VMEM((3 * wide, depth), bf16),
            pltpu.VMEM((span_rows, wide), f32),
            pltpu.VMEM((span_cols, wide), f32),
            pltpu.VMEM((ext_rows, DENSITIES * own), f32),
            pltpu.VMEM((ext_cols, DENSITIES * own), f32),
            pltpu.VMEM((DENSITIES * own, 3 * wide), bf16),
            pltpu.VMEM((wide, DENSITIES * own), bf16),
            pltpu.VMEM((wide, DENSITIES * own), bf16),
            pltpu.VMEM((DENSITIES, depth, depth), bf16),
            pltpu.VMEM((DENSITIES, DENSITIES, own, depth), bf16),
            pltpu.VMEM((DENSITIES * own, depth), bf16),
            pltpu.VMEM((DENSITIES * own, depth), f32),
            pltpu.VMEM((DENSITIES * own, depth), f32),
            pltpu.VMEM((DENSITIES * own, depth), bf16),
            pltpu.VMEM((DENSITIES * own, depth), bf16),
            pltpu.VMEM((ext_rows, ext_cols, depth), f32),
            pltpu.VMEM((ext_rows, reach, depth), f32),
            pltpu.VMEM((ext_rows, reach, depth), f32),
            pltpu.VMEM((reach, span_cols, depth), f32),
            pltpu.VMEM((reach, span_cols, depth), f32),
            pltpu.SemaphoreType.DMA((2,)),
            pltpu.SemaphoreType.DMA((8, chunks)),
            pltpu.SemaphoreType.DMA((8, chunks)),
            pltpu.SemaphoreType.DMA((8, halves)),
            pltpu.SemaphoreType.DMA((8, halves)),
        ],
        compiler_params=pltpu.CompilerParams(
            vmem_limit_bytes=60 << 20, collective_id=0, has_side_effects=True),
    )(tangent, hessian.reshape(DENSITIES, DENSITIES, own, depth), kernel_rows, kernel_cols, kernel_depth)


def solution(mesh):
    return jax.shard_map(
        per_device,
        mesh=mesh,
        in_specs=(P("gx", "gy", None), P(None, None, "gx", "gy", None), P(), P(), P()),
        out_specs=P("gx", "gy", None),
        check_vma=False,
    )
```
